512 devices in a mesh: kvh: 8 (over y), qh: 4 (over x_hi, core), req: 16 (over x_lo, z).
Axes of the slice: x: 4 (x_hi: 2, x_lo: 2; x = x_hi * 2 + x_lo), y: 8, z: 8, core: 2. Of those that a mesh axis runs over, the one named last changes fastest.
Arguments:
- queries: bfloat16 [32, 1024, 64, 128], P('req', None, ('kvh', 'qh')), may hold values from -12 to 12
- stretch_keys: bfloat16 [32, 1024, 8, 128], P('req', 'qh', 'kvh'), may hold values from -6 to 6
- stretch_values: bfloat16 [32, 1024, 8, 128], P('req', 'qh', 'kvh'), may hold values from -6 to 6
- cache_keys: bfloat16 [32, 1024, 8, 128], P('req', None, 'kvh'), may hold values from -6 to 6
- cache_values: bfloat16 [32, 1024, 8, 128], P('req', None, 'kvh'), may hold values from -6 to 6
- slot_of_req: int32 [32], replicated, may hold values from 0 to 31, each once
- cache_len: int32 [32], P('req'), may hold values from 128 to 1024, as said below
Outputs:
- attended: bfloat16 [32, 1024, 64, 128], P('req', None, ('kvh', 'qh'))
The draws below stay inside these ranges and needn't reach their ends.
Inputs may be any that keep to these rules, and one draw needn't show every extreme that they name: `cache_len`: one request in every draw has exactly 1024 cached positions.
All inputs are finite; a program needn't handle non-finite values.
Results may differ from the reference program's by a relative error of at most 0.0035.
Values may be sent and summed in bfloat16 or wider, within the bound.
A program may use at most 64 MiB of HBM per device.

```python
import jax
import jax.numpy as jnp
from jax import lax

H = 64
KVH = 8
HD = 128
STRETCH = 1024
CACHE_LEN = 1024
REQS = 32


def draw_queries(key, part):
    shape = (REQS, STRETCH, H, HD)
    base = jnp.clip(2.0 * jax.random.normal(jax.random.fold_in(key, 1), shape, jnp.float32), -12.0, 12.0)
    return base.astype(jnp.bfloat16)


def draw_cache_keys(key, part):
    shape = (REQS, CACHE_LEN, KVH, HD)
    base = jnp.clip(jax.random.normal(jax.random.fold_in(key, 2), shape, jnp.float32), -6.0, 6.0)
    return base.astype(jnp.bfloat16)


def draw_cache_len(key, part):
    lengths = jax.random.randint(jax.random.fold_in(key, 11), (REQS,), CACHE_LEN // 8, CACHE_LEN + 1, dtype=jnp.int32)
    longest = jax.random.randint(jax.random.fold_in(key, 12), (), 0, REQS, dtype=jnp.int32)
    return jnp.where(jnp.arange(REQS, dtype=jnp.int32) == longest, CACHE_LEN, lengths).astype(jnp.int32)


def steps_of(own_key, extent, shards, smallest, largest):
    def one(dim, shards_of):
        steps = jax.random.uniform(jax.random.fold_in(jax.random.fold_in(own_key, 6), dim), (shards_of,), jnp.float32, smallest / len(shards), largest / len(shards))
        return jnp.repeat(jnp.exp(steps), extent[dim] // shards_of).reshape((-1,) + (1,) * (len(extent) - dim - 1))

    gain = one(*shards[0])
    for cut in shards[1:]:
        gain = gain * one(*cut)
    return gain


def scatter_about(own_key, extent, deviation, most, cuts=(), held_as=jnp.bfloat16):
    level = steps_of(own_key, extent, cuts, -0.22, 0.18) if cuts else 1.0
    array = jax.random.normal(own_key, extent, jnp.float32) * deviation * level
    return jnp.minimum(jnp.maximum(array, -most), most).astype(held_as)


def setup_inputs(seed: int = 0) -> dict:
    key_list = jax.random.split(jax.random.key(seed), 8)
    return {
        "queries": draw_queries(jax.random.fold_in(key_list[7], 71), 0),
        "stretch_keys": scatter_about(key_list[1], (REQS, STRETCH, KVH, HD), 1.0, 6.0, ((0, 16), (1, 4), (2, 8))),
        "stretch_values": scatter_about(key_list[2], (REQS, STRETCH, KVH, HD), 1.0, 6.0, ((0, 16), (1, 4), (2, 8))),
        "cache_keys": draw_cache_keys(jax.random.fold_in(key_list[7], 71), 0),
        "cache_values": scatter_about(key_list[4], (REQS, CACHE_LEN, KVH, HD), 1.0, 6.0, ((0, 16), (2, 8))),
        "slot_of_req": jax.random.permutation(key_list[5], REQS).astype(jnp.int32),
        "cache_len": draw_cache_len(jax.random.fold_in(key_list[7], 71), 0),
    }


def attend_request(inputs):
    query, keys_cache, values_cache, keys_stretch, values_stretch, length = inputs
    group = H // KVH
    factor = HD ** -0.5

    def per_group(index):
        query_part = lax.dynamic_slice_in_dim(query, index * group, group, 1).astype(jnp.float32)
        key_c = lax.dynamic_index_in_dim(keys_cache, index, 1, keepdims=False).astype(jnp.float32)
        value_c = lax.dynamic_index_in_dim(values_cache, index, 1, keepdims=False).astype(jnp.float32)
        key_n = lax.dynamic_index_in_dim(keys_stretch, index, 1, keepdims=False).astype(jnp.float32)
        value_n = lax.dynamic_index_in_dim(values_stretch, index, 1, keepdims=False).astype(jnp.float32)
        score_c = jnp.einsum("thd,pd->htp", query_part, key_c) * factor
        score_n = jnp.einsum("thd,ud->htu", query_part, key_n) * factor
        seen_c = (jnp.arange(CACHE_LEN, dtype=jnp.int32) < length)[None, None, :]
        seen_n = (jnp.arange(STRETCH, dtype=jnp.int32)[None, :] <= jnp.arange(STRETCH, dtype=jnp.int32)[:, None])[None]
        top_c = jnp.max(jnp.where(seen_c, score_c, -jnp.inf), axis=2)
        top_n = jnp.max(jnp.where(seen_n, score_n, -jnp.inf), axis=2)
        top = jnp.maximum(top_c, top_n)[:, :, None]
        weight_c = jnp.where(seen_c, jnp.exp(score_c - top), 0.0)
        weight_n = jnp.where(seen_n, jnp.exp(score_n - top), 0.0)
        total = jnp.sum(weight_c, axis=2) + jnp.sum(weight_n, axis=2)
        rounded_c = lax.optimization_barrier(weight_c.astype(jnp.bfloat16)).astype(jnp.float32)
        rounded_n = lax.optimization_barrier(weight_n.astype(jnp.bfloat16)).astype(jnp.float32)
        mixed = jnp.einsum("htp,pd->thd", rounded_c, value_c) + jnp.einsum("htu,ud->thd", rounded_n, value_n)
        return (mixed / jnp.transpose(total)[:, :, None]).astype(jnp.bfloat16)

    outputs = lax.map(per_group, jnp.arange(KVH, dtype=jnp.int32))
    return jnp.transpose(outputs, (1, 0, 2, 3)).reshape(STRETCH, H, HD)


def reference(queries, stretch_keys, stretch_values, cache_keys, cache_values, slot_of_req, cache_len):
    cached_keys = jnp.take(cache_keys, slot_of_req, axis=0)
    cached_values = jnp.take(cache_values, slot_of_req, axis=0)
    return lax.map(attend_request, (queries, cached_keys, cached_values, stretch_keys, stretch_values, cache_len))
```

```python
import functools
import math

import jax
import jax.numpy as jnp
from jax import lax
from jax.experimental import pallas as pl
from jax.experimental.pallas import tpu as pltpu
from jax.sharding import PartitionSpec as P

MESH = pl.DeviceIdType.MESH
HIDDEN = -1e30


def move_kernel(
    n, slot_ref, sk_ref, sv_ref, ck_ref, cv_ref, skb, svb, kcb, vcb,
    spread, picked, local_sem, s_send, s_recv, p1_send, p1_recv, p2_send, p2_recv,
    x_send, x_recv, y_send, y_recv,
):
    me = lax.axis_index("req")
    q = lax.axis_index("qh")
    core = lax.rem(q, 2)
    side = q // 2
    mate = q + 1 - 2 * core
    over = lax.rem(q + 2, 4)
    per = sk_ref.shape[1]
    span = ck_ref.shape[1]
    half = span // 2
    piece = half // n

    barrier = pltpu.get_barrier_semaphore()

    def greet(d, _):
        pl.semaphore_signal(barrier, inc=1, device_id={"req": lax.rem(me + d, n)}, device_id_type=MESH)
        return 0

    lax.fori_loop(1, n, greet, 0)
    for peer in (mate, over):
        pl.semaphore_signal(barrier, inc=1, device_id={"qh": peer}, device_id_type=MESH)

    def rows_of(index, of_side):
        return pl.ds(pl.multiple_of(of_side * half + index * piece, piece), piece)

    own = pl.ds(pl.multiple_of(q * per, per), per)
    own_copies = [
        pltpu.make_async_copy(sk_ref, skb.at[:, own], local_sem.at[0]),
        pltpu.make_async_copy(sv_ref, svb.at[:, own], local_sem.at[1]),
    ]
    for copy in own_copies:
        copy.start()
    mine = pl.ds(2 * me, 2)
    for c, src in enumerate((ck_ref, cv_ref)):
        @pl.when(core == c)
        def _(src=src):
            pltpu.make_async_copy(src.at[:, rows_of(me, side)], spread.at[mine], local_sem.at[2]).start()

    pl.semaphore_wait(barrier, n + 1)

    for c, src in enumerate((ck_ref, cv_ref)):
        @pl.when(core == c)
        def _(src=src):
            def send(d, _):
                to = lax.rem(me + d, n)
                pltpu.make_async_remote_copy(
                    src.at[:, rows_of(to, side)], spread.at[mine], p1_send, p1_recv,
                    device_id={"req": to}, device_id_type=MESH,
                ).start()
                return 0

            lax.fori_loop(1, n, send, 0)

    def stretch(k, peer):
        return [
            pltpu.make_async_remote_copy(
                src, dst.at[:, own], s_send.at[k, i], s_recv.at[k, i],
                device_id={"qh": peer}, device_id_type=MESH,
            )
            for i, (src, dst) in enumerate(((sk_ref, skb), (sv_ref, svb)))
        ]

    to_over = stretch(0, over)
    to_mate = stretch(1, mate)
    for copy in to_over + to_mate:
        copy.start()

    pltpu.make_async_copy(spread.at[mine], spread.at[mine], local_sem.at[2]).wait()
    most = pl.ds(0, 2 * (n - 1))
    pltpu.make_async_copy(spread.at[most], spread.at[most], p1_recv).wait()
    for r in range(2 * n):
        picked[r] = spread[slot_ref[r]]

    for j in range(2):
        for c, dst in enumerate((kcb, vcb)):
            @pl.when(core == c)
            def _(j=j, dst=dst):
                def send(d, _):
                    to = lax.rem(me + d, n)
                    pltpu.make_async_remote_copy(
                        picked.at[2 * to + j], dst.at[j, rows_of(me, side)], p2_send, p2_recv.at[j, d],
                        device_id={"req": to}, device_id_type=MESH,
                    ).start()
                    return 0

                pltpu.make_async_copy(
                    picked.at[2 * me + j], dst.at[j, rows_of(me, side)], p2_recv.at[j, 0]
                ).start()
                lax.fori_loop(1, n, send, 0)

    theirs = pl.ds(pl.multiple_of(over * per, per), per)
    for copy in to_over:
        copy.wait_recv()
    passed = [
        pltpu.make_async_remote_copy(
            dst.at[:, theirs], dst.at[:, theirs], s_send.at[2, i], s_recv.at[2, i],
            device_id={"qh": mate}, device_id_type=MESH,
        )
        for i, dst in enumerate((skb, svb))
    ]
    for copy in passed:
        copy.start()

    def forward(dst, j, d):
        rows = rows_of(lax.rem(me + n - d, n), side)
        pltpu.make_async_copy(picked.at[0], dst.at[j, rows], p2_recv.at[j, d]).wait()
        pltpu.make_async_remote_copy(
            dst.at[j, rows], dst.at[j, rows], x_send, x_recv.at[j, d],
            device_id={"qh": over}, device_id_type=MESH,
        ).start()
        pltpu.make_async_remote_copy(
            dst.at[j, rows], dst.at[j, rows], y_send, y_recv,
            device_id={"qh": mate}, device_id_type=MESH,
        ).start()

    def onward(dst, j, d):
        rows = rows_of(lax.rem(me + n - d, n), 1 - side)
        pltpu.make_async_copy(picked.at[0], dst.at[j, rows], x_recv.at[j, d]).wait()
        pltpu.make_async_remote_copy(
            dst.at[j, rows], dst.at[j, rows], y_send, y_recv,
            device_id={"qh": mate}, device_id_type=MESH,
        ).start()

    for step in (forward, onward):
        for c, dst in enumerate((kcb, vcb)):
            @pl.when(core == c)
            def _(step=step, dst=dst):
                for j in range(2):
                    def body(d, _, j=j):
                        step(dst, j, d)
                        return 0

                    lax.fori_loop(0, n, body, 0)

    pltpu.make_async_copy(kcb, vcb, y_recv).wait()
    for copy in own_copies:
        copy.wait()
    for copy in to_mate:
        copy.wait()
    for copy in to_over:
        copy.wait_send()
    for copy in passed:
        copy.wait()
    pltpu.make_async_copy(spread.at[most], spread.at[most], p1_send).wait()
    pltpu.make_async_copy(spread.at[most], spread.at[most], p2_send).wait()
    pltpu.make_async_copy(spread, spread, x_send).wait()
    pltpu.make_async_copy(kcb, kcb, y_send).wait()


def move(slot_of_req, stretch_keys, stretch_values, cache_keys, cache_values, n):
    reqs, span, dim = cache_keys.shape
    full = jax.ShapeDtypeStruct((reqs, span, dim), cache_keys.dtype)
    piece = span // 2 // n
    any_spec = pl.BlockSpec(memory_space=pl.ANY)
    vmem = pl.BlockSpec(memory_space=pltpu.VMEM)
    dma = pltpu.SemaphoreType.DMA
    return pl.pallas_call(
        functools.partial(move_kernel, n),
        out_shape=(full,) * 4,
        in_specs=[pl.BlockSpec(memory_space=pltpu.SMEM)] + [any_spec] * 4,
        out_specs=(vmem,) * 4,
        scratch_shapes=[
            pltpu.VMEM((2 * n, piece, dim), cache_keys.dtype),
            pltpu.VMEM((2 * n, piece, dim), cache_keys.dtype),
            dma((3,)), dma((3, 2)), dma((3, 2)), dma, dma, dma, dma((2, n)),
            dma, dma((2, n)), dma, dma,
        ],
        compiler_params=pltpu.CompilerParams(collective_id=0, has_side_effects=True),
    )(slot_of_req, stretch_keys, stretch_values, cache_keys, cache_values)


def attend_kernel(len_ref, q_ref, skb, svb, kcb, vcb, o_ref):
    tile, dim = q_ref.shape[1:]
    span = kcb.shape[1]
    tokens = tile // 2
    r = pl.program_id(0)
    i = pl.program_id(1)
    scale = math.log2(math.e) / math.sqrt(dim)
    query = q_ref[0]
    ones = jnp.ones((tokens, dim), jnp.bfloat16)

    def block(carry, keys, values, seen):
        top, acc = carry
        scores = lax.dot_general(query, keys, (((1,), (1,)), ((), ())), preferred_element_type=jnp.float32)
        if seen is not None:
            scores = jnp.where(seen, scores, HIDDEN)
        new = jnp.maximum(top, jnp.max(scores, axis=1, keepdims=True))
        weights = jnp.exp2((scores - new) * scale).astype(jnp.bfloat16)
        wide = jnp.concatenate([values, ones], axis=1)
        acc = acc * jnp.exp2((top - new) * scale) + jnp.dot(weights, wide, preferred_element_type=jnp.float32)
        return new, acc

    def keys_at(ref, b):
        return ref[0, pl.ds(pl.multiple_of(b * tokens, tokens), tokens), :]

    row = lax.broadcasted_iota(jnp.int32, (tile, tokens), 0) // 2
    col = lax.broadcasted_iota(jnp.int32, (tile, tokens), 1)
    carry = (jnp.full((tile, 1), HIDDEN, jnp.float32), jnp.zeros((tile, 2 * dim), jnp.float32))
    carry = block(carry, keys_at(skb, i), keys_at(svb, i), col <= row)
    carry = lax.fori_loop(0, i, lambda b, c: block(c, keys_at(skb, b), keys_at(svb, b), None), carry)
    length = len_ref[r]
    whole = length // tokens
    carry = lax.fori_loop(0, whole, lambda b, c: block(c, keys_at(kcb, b), keys_at(vcb, b), None), carry)
    carry = lax.fori_loop(
        whole, pl.cdiv(length, tokens),
        lambda b, c: block(c, keys_at(kcb, b), keys_at(vcb, b), col < length - b * tokens), carry,
    )
    acc = carry[1]
    o_ref[0] = (acc[:, :dim] / acc[:, dim:]).astype(o_ref.dtype)


def attend(cache_len, queries, skb, svb, kcb, vcb):
    reqs, rows, dim = queries.shape
    tile = 512
    whole = pl.BlockSpec((1,) + skb.shape[1:], lambda r, i, *_: (r, 0, 0))
    tiled = pl.BlockSpec((1, tile, dim), lambda r, i, *_: (r, i, 0))
    return pl.pallas_call(
        attend_kernel,
        out_shape=jax.ShapeDtypeStruct(queries.shape, queries.dtype),
        grid_spec=pltpu.PrefetchScalarGridSpec(
            num_scalar_prefetch=1,
            grid=(reqs, rows // tile),
            in_specs=[tiled, whole, whole, whole, whole],
            out_specs=tiled,
        ),
        compiler_params=pltpu.CompilerParams(dimension_semantics=("arbitrary", "arbitrary")),
    )(cache_len, queries, skb, svb, kcb, vcb)


def on_device(queries, stretch_keys, stretch_values, cache_keys, cache_values, slot_of_req, cache_len):
    reqs, stretch, heads, dim = queries.shape
    flat = [a.reshape(a.shape[0], a.shape[1], dim) for a in (stretch_keys, stretch_values, cache_keys, cache_values)]
    moved = move(slot_of_req, *flat, lax.axis_size("req"))
    out = attend(cache_len, queries.reshape(reqs, stretch * heads, dim), *moved)
    return out.reshape(queries.shape)


def solution(mesh):
    return jax.shard_map(
        on_device,
        mesh=mesh,
        in_specs=(
            P("req", None, ("kvh", "qh"), None),
            P("req", "qh", "kvh", None),
            P("req", "qh", "kvh", None),
            P("req", None, "kvh", None),
            P("req", None, "kvh", None),
            P(),
            P("req"),
        ),
        out_specs=P("req", None, ("kvh", "qh"), None),
        check_vma=False,
    )
```

```python
import functools
import math

import jax
import jax.numpy as jnp
from jax import lax
from jax.experimental import pallas as pl
from jax.experimental.pallas import tpu as pltpu
from jax.sharding import PartitionSpec as P

MESH = pl.DeviceIdType.MESH
HIDDEN = -1e30
F32 = jnp.float32


def scores_of(query, keys):
    return lax.dot_general(query, keys, (((1,), (1,)), ((), ())), preferred_element_type=F32)


def kernel(
    n, slot_ref, len_ref, q_ref, sk_ref, sv_ref, ck_ref, cv_ref, out_ref,
    qv, qx, skb, svb, kcb, vcb, spread_a, spread_b, picked, kx, vx, acc, top, s0, s1, ov,
    local_sem, s_send, s_recv, p1_send, p1_recv, p2_send, p2_recv, x_send, x_recv, y_send, y_recv, out_sem,
):
    me = lax.axis_index("req")
    q = lax.axis_index("qh")
    core = lax.rem(q, 2)
    side = q // 2
    mate = q + 1 - 2 * core
    over = lax.rem(q + 2, 4)
    reqs, rows, dim = q_ref.shape
    per = sk_ref.shape[1]
    span = ck_ref.shape[1]
    half = span // 2
    part = half // 2
    piece = part // n
    depth = n // 2

    def shift(i):
        s = i // 2
        dz = lax.rem(depth // 2 + (s + 1) // 2 * (1 - 2 * lax.rem(s, 2)) + depth, depth)
        return 1 - lax.rem(i, 2), dz

    def target(i):
        dx, dz = shift(i)
        return lax.rem(me // depth + dx, 2) * depth + lax.rem(lax.rem(me, depth) + dz, depth)

    def source(i):
        dx, dz = shift(i)
        return lax.rem(me // depth + dx, 2) * depth + lax.rem(lax.rem(me, depth) + depth - dz, depth)

    def rows_of(h, of_side, index):
        return pl.ds(pl.multiple_of(h * half + of_side * part + index * piece, piece), piece)

    def pair(index):
        return pl.ds(2 * index, 2)

    def each_core(refs, body):
        for c, ref in enumerate(refs):
            @pl.when(core == c)
            def _(ref=ref):
                body(ref)

    def to_req(src, dst, send, recv, index):
        return pltpu.make_async_remote_copy(
            src, dst, send, recv, device_id={"req": index}, device_id_type=MESH
        )

    def to_qh(src, dst, send, recv, index):
        return pltpu.make_async_remote_copy(
            src, dst, send, recv, device_id={"qh": index}, device_id_type=MESH
        )

    spread = (spread_a, spread_b)
    barrier = pltpu.get_barrier_semaphore()

    def greet(i, _):
        pl.semaphore_signal(barrier, inc=1, device_id={"req": target(i)}, device_id_type=MESH)
        return 0

    lax.fori_loop(0, n - 1, greet, 0)
    for peer in (over, mate):
        pl.semaphore_signal(barrier, inc=1, device_id={"qh": peer}, device_id_type=MESH)

    own = pl.ds(pl.multiple_of(q * per, per), per)
    load_q = pltpu.make_async_copy(q_ref, qv, local_sem.at[0])
    own_copies = [
        pltpu.make_async_copy(sk_ref, skb.at[:, own], local_sem.at[1]),
        pltpu.make_async_copy(sv_ref, svb.at[:, own], local_sem.at[2]),
    ]

    pl.semaphore_wait(barrier, n + 1)

    def spread_out(src):
        for h in range(2):
            def send(i, _, h=h):
                to = target(i)
                to_req(
                    src.at[:, rows_of(h, side, to)], spread[h].at[pair(me)], p1_send, p1_recv.at[h], to
                ).start()
                return 0

            lax.fori_loop(0, n - 1, send, 0)
            pltpu.make_async_copy(
                src.at[:, rows_of(h, side, me)], spread[h].at[pair(me)], local_sem.at[3 + h]
            ).start()

    each_core((ck_ref, cv_ref), spread_out)

    def stretch_to(k, peer):
        return [
            to_qh(src, dst.at[:, own], s_send.at[k, i], s_recv.at[k, i], peer)
            for i, (src, dst) in enumerate(((sk_ref, skb), (sv_ref, svb)))
        ]

    to_over = stretch_to(0, over)
    to_mate = stretch_to(1, mate)
    for copy in to_over + to_mate + [load_q] + own_copies:
        copy.start()

    scale = math.log2(math.e) / math.sqrt(dim)
    load_q.wait()
    block = 256

    def widen(i, _):
        at = pl.ds(pl.multiple_of(i * block, block), block)
        for j in range(reqs):
            value = qv[j, at, :].astype(F32) * scale
            high = value.astype(jnp.bfloat16)
            qx[j, at, :dim] = high
            qx[j, at, dim:] = (value - high.astype(F32)).astype(jnp.bfloat16)
        return 0

    lax.fori_loop(0, rows // block, widen, 0)

    most = pl.ds(0, 2 * (n - 1))

    def collect(h):
        pltpu.make_async_copy(spread[h].at[pair(me)], spread[h].at[pair(me)], local_sem.at[3 + h]).wait()
        pltpu.make_async_copy(spread[h].at[most], spread[h].at[most], p1_recv.at[h]).wait()
        for r in range(2 * n):
            picked[h, r] = spread[h][slot_ref[r]]

        def send_all(dst):
            def send(i, _):
                to = target(i)
                to_req(
                    picked.at[h, pair(to)], dst.at[:, rows_of(h, side, me)], p2_send, p2_recv.at[h, i], to
                ).start()
                return 0

            lax.fori_loop(0, n - 1, send, 0)
            pltpu.make_async_copy(
                picked.at[h, pair(me)], dst.at[:, rows_of(h, side, me)], p2_recv.at[h, n - 1]
            ).start()

        each_core((kcb, vcb), send_all)

    def forward(h):
        def send_all(dst):
            def send(k, _):
                i = n - 1 - k
                at = rows_of(h, side, source(i))
                pltpu.make_async_copy(picked.at[h, pair(0)], dst.at[:, at], p2_recv.at[h, i]).wait()
                to_qh(dst.at[:, at], dst.at[:, at], x_send, x_recv.at[h, i], over).start()
                to_qh(dst.at[:, at], dst.at[:, at], y_send, y_recv.at[h], mate).start()
                return 0

            lax.fori_loop(0, n, send, 0)

        each_core((kcb, vcb), send_all)

    def onward(h):
        def send_all(dst):
            def send(k, _):
                i = n - 1 - k
                at = rows_of(h, 1 - side, source(i))
                pltpu.make_async_copy(picked.at[h, pair(0)], dst.at[:, at], x_recv.at[h, i]).wait()
                to_qh(dst.at[:, at], dst.at[:, at], y_send, y_recv.at[h], mate).start()
                return 0

            lax.fori_loop(0, n, send, 0)

        each_core((kcb, vcb), send_all)

    tile = 512
    tokens = tile // 2

    def stretch_attention(j):
        for i in range(rows // tile):
            at = pl.ds(i * tile, tile)
            seen = (i + 1) * tokens
            keys = skb[j, :seen, :]
            scores = scores_of(qx[j, at, :], jnp.concatenate([keys, keys], axis=1))
            row = lax.broadcasted_iota(jnp.int32, (tile, tokens), 0) // 2
            col = lax.broadcasted_iota(jnp.int32, (tile, tokens), 1)
            last = jnp.where(col <= row, scores[:, seen - tokens:], HIDDEN)
            scores = jnp.concatenate([scores[:, : seen - tokens], last], axis=1) if i else last
            most = jnp.max(scores, axis=1, keepdims=True)
            weights = jnp.exp2(scores - most).astype(jnp.bfloat16)
            values = svb[j, :seen, :]
            wide = jnp.concatenate([values, jnp.ones_like(values)], axis=1)
            acc[j, at, :] = jnp.dot(weights, wide, preferred_element_type=F32)
            top[j, at, :] = jnp.broadcast_to(most, (tile, dim))

    def prepare(h):
        for j in range(reqs):
            at = pl.ds(h * half, half)
            place = h * half + lax.broadcasted_iota(jnp.int32, (half, dim), 0)
            visible = place < len_ref[j]
            first = kcb[j, 0:1, :].astype(F32)
            keys = jnp.where(visible, kcb[j, at, :].astype(F32), first).astype(jnp.bfloat16)
            kx[j, :, :dim] = keys
            kx[j, :, dim:] = keys
            vx[j, :, :dim] = jnp.where(visible, vcb[j, at, :].astype(F32), 0.0).astype(jnp.bfloat16)
            vx[j, :, dim:] = jnp.where(visible, 1.0, 0.0).astype(jnp.bfloat16)

    big = 1024
    tiles = rows // big

    def place_of(t):
        return t // tiles, pl.ds(pl.multiple_of(lax.rem(t, tiles) * big, big), big)

    def cached_scores(t, dst):
        j, at = place_of(t)
        dst[...] = scores_of(qx[j, at, :], kx[j])

    def finish(t, src, last):
        j, at = place_of(t)
        scores = src[...]
        before = top[j, at, :]
        now = jnp.maximum(before, jnp.max(scores, axis=1, keepdims=True))
        weights = jnp.exp2(scores - now[:, :1]).astype(jnp.bfloat16)
        fade = jnp.exp2(before - now)
        mixed = jnp.dot(weights, vx[j], preferred_element_type=F32)
        number = acc[j, at, :dim] * fade + mixed[:, :dim]
        total = acc[j, at, dim:] * fade + mixed[:, dim:]
        if last:
            ov[j, at, :] = (number / total).astype(ov.dtype)
        else:
            acc[j, at, :dim] = number
            acc[j, at, dim:] = total
            top[j, at, :] = now

    def cached_attention(h, between=None):
        count = reqs * tiles
        bufs = (s0, s1)
        cached_scores(0, s0)
        for t in range(count):
            if t + 1 < count:
                cached_scores(t + 1, bufs[(t + 1) % 2])
            finish(t, bufs[t % 2], h == 1)
            if between is not None and t == count // 2 - 1:
                between()
            if h == 1:
                j, at = t // tiles, pl.ds(t % tiles * big, big)
                pltpu.make_async_copy(ov.at[j, at], out_ref.at[j, at], out_sem).start()

    collect(0)
    for copy in to_over:
        copy.wait_recv()
    theirs = pl.ds(pl.multiple_of(over * per, per), per)
    passed = [
        to_qh(dst.at[:, theirs], dst.at[:, theirs], s_send.at[2, i], s_recv.at[2, i], mate)
        for i, dst in enumerate((skb, svb))
    ]
    for copy in passed:
        copy.start()
    collect(1)
    for copy in own_copies:
        copy.wait()
    for copy in to_mate + passed:
        copy.wait_recv()
    stretch_attention(0)
    forward(0)
    stretch_attention(1)
    onward(0)
    forward(1)
    firsts = pl.ds(0, half)
    pltpu.make_async_copy(kcb.at[:, firsts], vcb.at[:, firsts], y_recv.at[0]).wait()
    prepare(0)
    cached_attention(0, lambda: onward(1))
    pltpu.make_async_copy(kcb.at[:, firsts], vcb.at[:, firsts], y_recv.at[1]).wait()
    prepare(1)
    cached_attention(1)

    for copy in to_over + to_mate + passed:
        copy.wait_send()
    for sem in (p1_send, p2_send):
        pltpu.make_async_copy(picked.at[:, most], picked.at[:, most], sem).wait()
    pltpu.make_async_copy(picked, picked, x_send).wait()
    pltpu.make_async_copy(kcb, kcb, y_send).wait()
    pltpu.make_async_copy(ov, out_ref, out_sem).wait()


def attend(slot_of_req, cache_len, queries, stretch_keys, stretch_values, cache_keys, cache_values, n):
    reqs, rows, dim = queries.shape
    span = cache_keys.shape[1]
    half = span // 2
    piece = half // 2 // n
    kind = queries.dtype
    any_spec = pl.BlockSpec(memory_space=pl.ANY)
    smem = pl.BlockSpec(memory_space=pltpu.SMEM)
    dma = pltpu.SemaphoreType.DMA
    vmem = pltpu.VMEM
    return pl.pallas_call(
        functools.partial(kernel, n),
        out_shape=jax.ShapeDtypeStruct(queries.shape, kind),
        in_specs=[smem] * 2 + [any_spec] * 5,
        out_specs=any_spec,
        scratch_shapes=[
            vmem((reqs, rows, dim), kind),
            vmem((reqs, rows, 2 * dim), kind),
            vmem((reqs, span, dim), kind), vmem((reqs, span, dim), kind),
            vmem((reqs, span, dim), kind), vmem((reqs, span, dim), kind),
            vmem((2 * n, piece, dim), kind), vmem((2 * n, piece, dim), kind), vmem((2, 2 * n, piece, dim), kind),
            vmem((reqs, half, 2 * dim), kind), vmem((reqs, half, 2 * dim), kind),
            vmem((reqs, rows, 2 * dim), F32), vmem((reqs, rows, dim), F32),
            vmem((1024, half), F32), vmem((1024, half), F32),
            vmem((reqs, rows, dim), kind),
            dma((5,)), dma((3, 2)), dma((3, 2)), dma, dma((2,)), dma, dma((2, n)),
            dma, dma((2, n)), dma, dma((2,)), dma,
        ],
        compiler_params=pltpu.CompilerParams(collective_id=0, has_side_effects=True),
    )(slot_of_req, cache_len, queries, stretch_keys, stretch_values, cache_keys, cache_values)


def on_device(queries, stretch_keys, stretch_values, cache_keys, cache_values, slot_of_req, cache_len):
    reqs, stretch, heads, dim = queries.shape
    flat = [a.reshape(a.shape[0], a.shape[1], dim) for a in (stretch_keys, stretch_values, cache_keys, cache_values)]
    rows = queries.reshape(reqs, stretch * heads, dim)
    out = attend(slot_of_req, cache_len, rows, *flat, lax.axis_size("req"))
    return out.reshape(queries.shape)


def solution(mesh):
    return jax.shard_map(
        on_device,
        mesh=mesh,
        in_specs=(
            P("req", None, ("kvh", "qh"), None),
            P("req", "qh", "kvh", None),
            P("req", "qh", "kvh", None),
            P("req", None, "kvh", None),
            P("req", None, "kvh", None),
            P(),
            P("req"),
        ),
        out_specs=P("req", None, ("kvh", "qh"), None),
        check_vma=False,
    )
```

```python
import functools
import math

import jax
import jax.numpy as jnp
from jax import lax
from jax.experimental import pallas as pl
from jax.experimental.pallas import tpu as pltpu
from jax.sharding import PartitionSpec as P

MESH = pl.DeviceIdType.MESH
HIDDEN = -1e30
F32 = jnp.float32


def scores_of(query, keys):
    return lax.dot_general(query, keys, (((1,), (1,)), ((), ())), preferred_element_type=F32)


def prepare(h, j, len_ref, kvb, kx, vx):
    half, dim = kx.shape[1], kx.shape[2] // 2
    at = pl.ds(h * half, half)
    place = h * half + lax.broadcasted_iota(jnp.int32, (half, dim), 0)
    visible = place < len_ref[j]
    first = kvb[0, j, 0:1, :].astype(F32)
    keys = jnp.where(visible, kvb[0, j, at, :].astype(F32), first).astype(jnp.bfloat16)
    kx[j, :, :dim] = keys
    kx[j, :, dim:] = keys
    vx[j, :, :dim] = jnp.where(visible, kvb[1, j, at, :].astype(F32), 0.0).astype(jnp.bfloat16)
    vx[j, :, dim:] = jnp.where(visible, 1.0, 0.0).astype(jnp.bfloat16)


def join(scores, before, values):
    now = jnp.maximum(before, jnp.max(scores, axis=1, keepdims=True))
    weights = jnp.exp2(scores - now[:, :1]).astype(jnp.bfloat16)
    return now, jnp.exp2(before - now), jnp.dot(weights, values, preferred_element_type=F32)


def kernel(
    n, slot_ref, len_ref, q_ref, sk_ref, sv_ref, ck_ref, cv_ref, qx, acc, top, kvb,
    qv, skb, svb, spread_a, spread_b, picked, kx, vx, s0, s1,
    local_sem, s_send, s_recv, p1_send, p1_recv, p2_send, p2_recv, x_send, x_recv, y_send, y_recv,
):
    me = lax.axis_index("req")
    q = lax.axis_index("qh")
    core = lax.rem(q, 2)
    side = q // 2
    mate = q + 1 - 2 * core
    over = lax.rem(q + 2, 4)
    reqs, rows, dim = q_ref.shape
    per = sk_ref.shape[1]
    span = ck_ref.shape[1]
    half = span // 2
    part = half // 2
    piece = part // n
    depth = n // 2

    far = sorted(range(depth), key=lambda dz: -min(dz, depth - dz))
    offsets = [(dx, dz) for dz in far for dx in (1, 0) if dx or dz]
    all_offsets = offsets + [(0, 0)]
    here = side * 2 + me // depth
    up = here + 1 - 2 * lax.rem(here, 2)
    down = lax.rem(here + 3 + 2 * lax.rem(here, 2), 4)
    columns = [(x // 2, lax.rem(x, 2) * depth) for x in (here, up, down)]
    heights = [lax.rem(lax.rem(me, depth) + dz, depth) for dz in range(depth)]

    def partner(offset, sign):
        dx, dz = offset
        of_side, base = columns[dx * (1 + dz % 2)]
        return of_side, base + heights[sign * dz % depth]

    def rows_of(h, of_side, index):
        return pl.ds(pl.multiple_of(h * half + of_side * part + index * piece, piece), piece)

    def pair(index):
        return pl.ds(2 * index, 2)

    def to_req(src, dst, send, recv, of_side, index):
        return pltpu.make_async_remote_copy(
            src, dst, send, recv, device_id={"qh": of_side * 2 + core, "req": index}, device_id_type=MESH
        )

    def to_qh(src, dst, send, recv, index):
        return pltpu.make_async_remote_copy(
            src, dst, send, recv, device_id={"qh": index}, device_id_type=MESH
        )

    spread = (spread_a, spread_b)
    barrier = pltpu.get_barrier_semaphore()
    for offset in offsets:
        of_side, index = partner(offset, 1)
        pl.semaphore_signal(
            barrier, inc=1, device_id={"qh": of_side * 2 + core, "req": index}, device_id_type=MESH
        )
    for peer in (over, mate):
        pl.semaphore_signal(barrier, inc=1, device_id={"qh": peer}, device_id_type=MESH)

    own = pl.ds(pl.multiple_of(q * per, per), per)
    load_q = pltpu.make_async_copy(q_ref, qv, local_sem.at[0])
    own_copies = [
        pltpu.make_async_copy(sk_ref, skb.at[:, own], local_sem.at[1]),
        pltpu.make_async_copy(sv_ref, svb.at[:, own], local_sem.at[2]),
    ]

    pl.semaphore_wait(barrier, n + 1)

    for c, src in enumerate((ck_ref, cv_ref)):
        @pl.when(core == c)
        def _(src=src):
            for h in range(2):
                for offset in offsets:
                    of_side, to = partner(offset, 1)
                    to_req(
                        src.at[:, rows_of(h, of_side, to)], spread[h].at[pair(me)], p1_send, p1_recv.at[h],
                        of_side, to,
                    ).start()
                pltpu.make_async_copy(
                    src.at[:, rows_of(h, side, me)], spread[h].at[pair(me)], local_sem.at[3 + h]
                ).start()

    def stretch_to(k, peer):
        return [
            to_qh(src, dst.at[:, own], s_send.at[k, i], s_recv.at[k, i], peer)
            for i, (src, dst) in enumerate(((sk_ref, skb), (sv_ref, svb)))
        ]

    to_over = stretch_to(0, over)
    to_mate = stretch_to(1, mate)
    for copy in to_over + to_mate + [load_q] + own_copies:
        copy.start()

    scale = math.log2(math.e) / math.sqrt(dim)
    load_q.wait()
    block = 256

    def widen(i, _):
        at = pl.ds(pl.multiple_of(i * block, block), block)
        for j in range(reqs):
            value = qv[j, at, :].astype(F32) * scale
            high = value.astype(jnp.bfloat16)
            qx[j, at, :dim] = high
            qx[j, at, dim:] = (value - high.astype(F32)).astype(jnp.bfloat16)
        return 0

    lax.fori_loop(0, rows // block, widen, 0)

    most = pl.ds(0, 2 * (n - 1))

    def collect(h):
        pltpu.make_async_copy(spread[h].at[pair(me)], spread[h].at[pair(me)], local_sem.at[3 + h]).wait()
        pltpu.make_async_copy(spread[h].at[most], spread[h].at[most], p1_recv.at[h]).wait()
        for r in range(2 * n):
            picked[h, r] = spread[h][slot_ref[r]]
        dst = kvb.at[core, :, rows_of(h, side, me)]
        for i, offset in enumerate(offsets):
            of_side, to = partner(offset, 1)
            to_req(picked.at[h, pair(to)], dst, p2_send, p2_recv.at[h, i], of_side, to).start()
        pltpu.make_async_copy(picked.at[h, pair(me)], dst, p2_recv.at[h, n - 1]).start()

    def forward(h):
        for i in reversed(range(n)):
            of_side, index = partner(all_offsets[i], -1)
            at = kvb.at[core, :, rows_of(h, of_side, index)]
            pltpu.make_async_copy(picked.at[h, pair(0)], at, p2_recv.at[h, i]).wait()
            to_qh(at, at, x_send, x_recv.at[h, i], over).start()
            to_qh(at, at, y_send, y_recv.at[h], mate).start()

    def onward(h):
        for i in reversed(range(n)):
            of_side, index = partner(all_offsets[i], -1)
            at = kvb.at[core, :, rows_of(h, 1 - of_side, index)]
            pltpu.make_async_copy(picked.at[h, pair(0)], at, x_recv.at[h, i]).wait()
            to_qh(at, at, y_send, y_recv.at[h], mate).start()

    tile = 512
    tokens = tile // 2

    def stretch_attention(j):
        for i in range(rows // tile):
            at = pl.ds(i * tile, tile)
            seen = (i + 1) * tokens
            keys = skb[j, :seen, :]
            scores = scores_of(qx[j, at, :], jnp.concatenate([keys, keys], axis=1))
            row = lax.broadcasted_iota(jnp.int32, (tile, tokens), 0) // 2
            col = lax.broadcasted_iota(jnp.int32, (tile, tokens), 1)
            last = jnp.where(col <= row, scores[:, seen - tokens:], HIDDEN)
            scores = jnp.concatenate([scores[:, : seen - tokens], last], axis=1) if i else last
            highest = jnp.max(scores, axis=1, keepdims=True)
            weights = jnp.exp2(scores - highest).astype(jnp.bfloat16)
            values = svb[j, :seen, :]
            wide = jnp.concatenate([values, jnp.ones_like(values)], axis=1)
            acc[j, at, :] = jnp.dot(weights, wide, preferred_element_type=F32)
            top[j, at, :] = jnp.broadcast_to(highest, (tile, dim))

    big = 1024
    count = reqs * rows // big

    def place_of(t):
        return t // (rows // big), pl.ds(t % (rows // big) * big, big)

    def cached_scores(t):
        j, at = place_of(t)
        (s0, s1)[t % 2][...] = scores_of(qx[j, at, :], kx[j])

    def cached_attention(first, stop):
        for t in range(first, stop):
            if t + 1 < count:
                cached_scores(t + 1)
            j, at = place_of(t)
            now, fade, mixed = join((s0, s1)[t % 2][...], top[j, at, :], vx[j])
            acc[j, at, :dim] = acc[j, at, :dim] * fade + mixed[:, :dim]
            acc[j, at, dim:] = acc[j, at, dim:] * fade + mixed[:, dim:]
            top[j, at, :] = now

    collect(0)
    for copy in to_over:
        copy.wait_recv()
    theirs = pl.ds(pl.multiple_of(over * per, per), per)
    passed = [
        to_qh(dst.at[:, theirs], dst.at[:, theirs], s_send.at[2, i], s_recv.at[2, i], mate)
        for i, dst in enumerate((skb, svb))
    ]
    for copy in passed:
        copy.start()
    collect(1)
    for copy in own_copies:
        copy.wait()
    for copy in to_mate + passed:
        copy.wait_recv()
    stretch_attention(0)
    forward(0)
    stretch_attention(1)
    forward(1)
    onward(0)
    firsts = pl.ds(0, half)
    pltpu.make_async_copy(kvb.at[0, :, firsts], kvb.at[0, :, firsts], y_recv.at[0]).wait()
    for j in range(reqs):
        prepare(0, j, len_ref, kvb, kx, vx)
    cached_scores(0)
    cached_attention(0, count // 2)
    onward(1)
    cached_attention(count // 2, count)
    pltpu.make_async_copy(kvb.at[0, :, firsts], kvb.at[0, :, firsts], y_recv.at[1]).wait()

    for copy in to_over + to_mate + passed:
        copy.wait_send()
    for sem in (p1_send, p2_send):
        pltpu.make_async_copy(picked.at[:, most], picked.at[:, most], sem).wait()
    pltpu.make_async_copy(picked, picked, x_send).wait()
    pltpu.make_async_copy(kvb.at[0], kvb.at[0], y_send).wait()


def finish_kernel(len_ref, qx, acc, top, kvb, out_ref, kx, vx, s0, s1, ov, sem):
    reqs, rows, dim = ov.shape
    half = kx.shape[1]
    tile = 512
    bufs = (s0, s1)
    for j in range(reqs):
        def scores(t, j=j):
            bufs[t % 2][...] = scores_of(qx[j, pl.ds(t * tile, tile), :], kx[j])

        def put(at, number, total, j=j):
            ov[j, at, :] = (number / total).astype(ov.dtype)
            pltpu.make_async_copy(ov.at[j, at], out_ref.at[j, at], sem).start()

        @pl.when(len_ref[j] > half)
        def _(j=j, scores=scores, put=put):
            prepare(1, j, len_ref, kvb, kx, vx)
            scores(0)
            for t in range(rows // tile):
                if t + 1 < rows // tile:
                    scores(t + 1)
                at = pl.ds(t * tile, tile)
                _, fade, mixed = join(bufs[t % 2][...], top[j, at, :], vx[j])
                put(at, acc[j, at, :dim] * fade + mixed[:, :dim], acc[j, at, dim:] * fade + mixed[:, dim:])

        @pl.when(len_ref[j] <= half)
        def _(j=j, put=put):
            for t in range(rows // tile):
                at = pl.ds(t * tile, tile)
                put(at, acc[j, at, :dim], acc[j, at, dim:])

    pltpu.make_async_copy(ov, out_ref, sem).wait()


def attend(slot_of_req, cache_len, queries, stretch_keys, stretch_values, cache_keys, cache_values, n):
    reqs, rows, dim = queries.shape
    span = cache_keys.shape[1]
    half = span // 2
    piece = half // 2 // n
    kind = queries.dtype
    any_spec = pl.BlockSpec(memory_space=pltpu.HBM)
    smem = pl.BlockSpec(memory_space=pltpu.SMEM)
    dma = pltpu.SemaphoreType.DMA
    vmem = pltpu.VMEM
    held = pl.BlockSpec(memory_space=vmem)
    state = (
        vmem((reqs, rows, 2 * dim), kind),
        vmem((reqs, rows, 2 * dim), F32), vmem((reqs, rows, dim), F32),
        vmem((2, reqs, span, dim), kind),
    )
    limit = 57_600_000
    state = pl.pallas_call(
        functools.partial(kernel, n),
        out_shape=state,
        in_specs=[smem] * 2 + [any_spec] * 5,
        out_specs=(held,) * len(state),
        scratch_shapes=[
            vmem((reqs, rows, dim), kind),
            vmem((reqs, span, dim), kind), vmem((reqs, span, dim), kind),
            vmem((2 * n, piece, dim), kind), vmem((2 * n, piece, dim), kind), vmem((2, 2 * n, piece, dim), kind),
            vmem((reqs, half, 2 * dim), kind), vmem((reqs, half, 2 * dim), kind),
            vmem((1024, half), F32), vmem((1024, half), F32),
            dma((5,)), dma((3, 2)), dma((3, 2)), dma, dma((2,)), dma, dma((2, n)),
            dma, dma((2, n)), dma, dma((2,)),
        ],
        compiler_params=pltpu.CompilerParams(collective_id=0, has_side_effects=True, vmem_limit_bytes=limit),
    )(slot_of_req, cache_len, queries, stretch_keys, stretch_values, cache_keys, cache_values)
    state = [pltpu.with_memory_space_constraint(a, vmem) for a in state]
    return pl.pallas_call(
        finish_kernel,
        out_shape=jax.ShapeDtypeStruct(queries.shape, kind),
        in_specs=[smem] + [held] * len(state),
        out_specs=any_spec,
        scratch_shapes=[
            vmem((reqs, half, 2 * dim), kind), vmem((reqs, half, 2 * dim), kind),
            vmem((512, half), F32), vmem((512, half), F32),
            vmem((reqs, rows, dim), kind), dma,
        ],
        compiler_params=pltpu.CompilerParams(vmem_limit_bytes=limit),
    )(cache_len, *state)


def on_device(queries, stretch_keys, stretch_values, cache_keys, cache_values, slot_of_req, cache_len):
    reqs, stretch, heads, dim = queries.shape
    flat = [a.reshape(a.shape[0], a.shape[1], dim) for a in (stretch_keys, stretch_values, cache_keys, cache_values)]
    rows = queries.reshape(reqs, stretch * heads, dim)
    out = attend(slot_of_req, cache_len, rows, *flat, lax.axis_size("req"))
    return out.reshape(queries.shape)


def solution(mesh):
    return jax.shard_map(
        on_device,
        mesh=mesh,
        in_specs=(
            P("req", None, ("kvh", "qh"), None),
            P("req", "qh", "kvh", None),
            P("req", "qh", "kvh", None),
            P("req", None, "kvh", None),
            P("req", None, "kvh", None),
            P(),
            P("req"),
        ),
        out_specs=P("req", None, ("kvh", "qh"), None),
        check_vma=False,
    )
```

```python
import functools
import math

import jax
import jax.numpy as jnp
from jax import lax
from jax.experimental import pallas as pl
from jax.experimental.pallas import tpu as pltpu
from jax.sharding import PartitionSpec as P

MESH = pl.DeviceIdType.MESH
HIDDEN = -1e30
F32 = jnp.float32


CHUNKS = (4, 2, 2)


def scores_of(query, keys):
    return lax.dot_general(query, keys, (((1,), (1,)), ((), ())), preferred_element_type=F32)


def mark(start, j, len_ref, vx):
    size, dim = vx.shape[1], vx.shape[2] // 2
    place = start + lax.broadcasted_iota(jnp.int32, (size, dim), 0)
    vx[j, :, dim:] = jnp.where(place < len_ref[j], 1.0, 0.0).astype(jnp.bfloat16)


def prepare(start, j, kvb, kx, vx):
    size, dim = kx.shape[1], kx.shape[2] // 2
    at = pl.ds(start, size)
    visible = vx[j, :, dim:]
    keys = kvb[0, j, at, :] * visible + kvb[0, j, 0:1, :] * (1 - visible)
    kx[j, :, :dim] = keys
    kx[j, :, dim:] = keys
    vx[j, :, :dim] = kvb[1, j, at, :] * visible


def join(scores, before, values):
    now = jnp.maximum(before, jnp.max(scores, axis=1, keepdims=True))
    wide = jnp.concatenate([now] * (scores.shape[1] // now.shape[1]), axis=1)
    weights = jnp.exp2(scores - wide).astype(jnp.bfloat16)
    return now, jnp.exp2(before - now), jnp.dot(weights, values, preferred_element_type=F32)


def kernel(
    n, slot_ref, len_ref, q_ref, sk_ref, sv_ref, ck_ref, cv_ref, qx, acc, top, kvb,
    qv, skb, svb, s0, s1, spread, picked, kx, vx,
    local_sem, own_sem, s_send, s_recv, p1_send, p1_recv, p2_send, p2_recv, x_send, x_recv, y_send, y_recv,
):
    me = lax.axis_index("req")
    q = lax.axis_index("qh")
    core = lax.rem(q, 2)
    side = q // 2
    mate = q + 1 - 2 * core
    over = lax.rem(q + 2, 4)
    reqs, rows, dim = q_ref.shape
    per = sk_ref.shape[1]
    span = ck_ref.shape[1]
    sizes = [span // 8 * c for c in CHUNKS]
    starts = [sum(sizes[:h]) for h in range(len(sizes))]
    chunks = range(len(sizes))
    depth = n // 2

    far = sorted(range(depth), key=lambda dz: -min(dz, depth - dz))
    offsets = [(dx, dz) for dz in far for dx in (1, 0) if dx or dz]
    all_offsets = offsets + [(0, 0)]
    here = side * 2 + me // depth
    up = here + 1 - 2 * lax.rem(here, 2)
    down = lax.rem(here + 3 + 2 * lax.rem(here, 2), 4)
    columns = [(x // 2, lax.rem(x, 2) * depth) for x in (here, up, down)]
    heights = [lax.rem(lax.rem(me, depth) + dz, depth) for dz in range(depth)]

    def partner(offset, sign):
        dx, dz = offset
        of_side, base = columns[dx * (1 + dz % 2)]
        return of_side, base + heights[sign * dz % depth]

    def rows_of(h, of_side, index):
        piece = sizes[h] // 2 // n
        return pl.ds(pl.multiple_of(starts[h] + (of_side * n + index) * piece, piece), piece)

    def pair(index):
        return pl.ds(2 * index, 2)

    def to_req(src, dst, send, recv, of_side, index):
        return pltpu.make_async_remote_copy(
            src, dst, send, recv, device_id={"qh": of_side * 2 + core, "req": index}, device_id_type=MESH
        )

    def to_qh(src, dst, send, recv, index):
        return pltpu.make_async_remote_copy(
            src, dst, send, recv, device_id={"qh": index}, device_id_type=MESH
        )

    barrier = pltpu.get_barrier_semaphore()
    for offset in offsets:
        of_side, index = partner(offset, 1)
        pl.semaphore_signal(
            barrier, inc=1, device_id={"qh": of_side * 2 + core, "req": index}, device_id_type=MESH
        )
    for peer in (over, mate):
        pl.semaphore_signal(barrier, inc=1, device_id={"qh": peer}, device_id_type=MESH)

    own = pl.ds(pl.multiple_of(q * per, per), per)
    load_q = pltpu.make_async_copy(q_ref, qv, local_sem.at[0])
    own_copies = [
        pltpu.make_async_copy(sk_ref, skb.at[:, own], local_sem.at[1]),
        pltpu.make_async_copy(sv_ref, svb.at[:, own], local_sem.at[2]),
    ]

    pl.semaphore_wait(barrier, n + 1)

    for c, src in enumerate((ck_ref, cv_ref)):
        @pl.when(core == c)
        def _(src=src):
            for h in chunks:
                for offset in offsets:
                    of_side, to = partner(offset, 1)
                    to_req(
                        src.at[:, rows_of(h, of_side, to)], spread[h].at[pair(me)], p1_send.at[h], p1_recv.at[h],
                        of_side, to,
                    ).start()
                pltpu.make_async_copy(
                    src.at[:, rows_of(h, side, me)], spread[h].at[pair(me)], own_sem.at[h]
                ).start()

    def stretch_to(k, peer):
        return [
            to_qh(src, dst.at[:, own], s_send.at[k, i], s_recv.at[k, i], peer)
            for i, (src, dst) in enumerate(((sk_ref, skb), (sv_ref, svb)))
        ]

    to_over = stretch_to(0, over)
    to_mate = stretch_to(1, mate)
    for copy in to_over + to_mate + [load_q] + own_copies:
        copy.start()

    scale = math.log2(math.e) / math.sqrt(dim)
    load_q.wait()
    block = 256

    def widen(i, _):
        at = pl.ds(pl.multiple_of(i * block, block), block)
        for j in range(reqs):
            value = qv[j, at, :].astype(F32) * scale
            high = value.astype(jnp.bfloat16)
            qx[j, at, :dim] = high
            qx[j, at, dim:] = (value - high.astype(F32)).astype(jnp.bfloat16)
        return 0

    lax.fori_loop(0, rows // block, widen, 0)

    most = pl.ds(0, 2 * (n - 1))

    def collect(h):
        pltpu.make_async_copy(spread[h].at[pair(me)], spread[h].at[pair(me)], own_sem.at[h]).wait()
        pltpu.make_async_copy(spread[h].at[most], spread[h].at[most], p1_recv.at[h]).wait()
        for r in range(2 * n):
            picked[h][r] = spread[h][slot_ref[r]]
        dst = kvb.at[core, :, rows_of(h, side, me)]
        for i, offset in enumerate(offsets):
            of_side, to = partner(offset, 1)
            to_req(picked[h].at[pair(to)], dst, p2_send.at[h], p2_recv.at[h, i], of_side, to).start()
        pltpu.make_async_copy(picked[h].at[pair(me)], dst, p2_recv.at[h, n - 1]).start()

    def forward(h):
        for i in reversed(range(n)):
            of_side, index = partner(all_offsets[i], -1)
            at = kvb.at[core, :, rows_of(h, of_side, index)]
            pltpu.make_async_copy(picked[h].at[pair(0)], at, p2_recv.at[h, i]).wait()
            to_qh(at, at, x_send.at[h], x_recv.at[h, i], over).start()
            to_qh(at, at, y_send, y_recv.at[h], mate).start()

    def onward(h):
        for i in reversed(range(n)):
            of_side, index = partner(all_offsets[i], -1)
            at = kvb.at[core, :, rows_of(h, 1 - of_side, index)]
            pltpu.make_async_copy(picked[h].at[pair(0)], at, x_recv.at[h, i]).wait()
            to_qh(at, at, y_send, y_recv.at[h], mate).start()

    tile = 512
    tokens = tile // 2

    def stretch_attention(j):
        for i in range(rows // tile):
            at = pl.ds(i * tile, tile)
            seen = (i + 1) * tokens
            keys = skb[j, :seen, :]
            scores = scores_of(qx[j, at, :], jnp.concatenate([keys, keys], axis=1))
            row = lax.broadcasted_iota(jnp.int32, (tile, tokens), 0) // 2
            col = lax.broadcasted_iota(jnp.int32, (tile, tokens), 1)
            last = jnp.where(col <= row, scores[:, seen - tokens:], HIDDEN)
            scores = jnp.concatenate([scores[:, : seen - tokens], last], axis=1) if i else last
            highest = jnp.max(scores, axis=1, keepdims=True)
            weights = jnp.exp2(scores - highest).astype(jnp.bfloat16)
            values = svb[j, :seen, :]
            wide = jnp.concatenate([values, jnp.ones_like(values)], axis=1)
            acc[j, at, :] = jnp.dot(weights, wide, preferred_element_type=F32)
            top[j, at, :] = jnp.broadcast_to(highest, (tile, dim))

    big = 1024
    count = reqs * rows // big

    def place_of(t):
        return t // (rows // big), pl.ds(t % (rows // big) * big, big)

    def cached_scores(h, t):
        j, at = place_of(t)
        (s0, s1)[t % 2][:, : sizes[h]] = scores_of(qx[j, at, :], kx[h][j])

    def cached_attention(h, first, stop):
        for t in range(first, stop):
            if t + 1 < count:
                cached_scores(h, t + 1)
            j, at = place_of(t)
            now, fade, mixed = join((s0, s1)[t % 2][:, : sizes[h]], top[j, at, :], vx[h][j])
            acc[j, at, :dim] = acc[j, at, :dim] * fade + mixed[:, :dim]
            acc[j, at, dim:] = acc[j, at, dim:] * fade + mixed[:, dim:]
            top[j, at, :] = now

    for h in chunks[:-1]:
        for j in range(reqs):
            mark(starts[h], j, len_ref, vx[h])
    collect(0)
    for copy in to_over:
        copy.wait_recv()
    theirs = pl.ds(pl.multiple_of(over * per, per), per)
    passed = [
        to_qh(dst.at[:, theirs], dst.at[:, theirs], s_send.at[2, i], s_recv.at[2, i], mate)
        for i, dst in enumerate((skb, svb))
    ]
    for copy in passed:
        copy.start()
    for h in chunks[1:]:
        collect(h)
    for copy in own_copies:
        copy.wait()
    for copy in to_mate + passed:
        copy.wait_recv()
    stretch_attention(0)
    forward(0)
    stretch_attention(1)
    for h in chunks[1:]:
        forward(h)
    onward(0)
    for h in chunks:
        landed = kvb.at[0, :, pl.ds(starts[h], sizes[h])]
        pltpu.make_async_copy(landed, landed, y_recv.at[h]).wait()
        if h == chunks[-1]:
            break
        for j in range(reqs):
            prepare(starts[h], j, kvb, kx[h], vx[h])
        cached_scores(h, 0)
        cached_attention(h, 0, count // 2)
        onward(h + 1)
        cached_attention(h, count // 2, count)

    for copy in to_over + to_mate + passed:
        copy.wait_send()
    for sem in (p1_send, p2_send):
        for h in chunks:
            pltpu.make_async_copy(picked[h].at[most], picked[h].at[most], sem.at[h]).wait()
    for h in chunks:
        pltpu.make_async_copy(picked[h], picked[h], x_send.at[h]).wait()
    pltpu.make_async_copy(kvb.at[0], kvb.at[0], y_send).wait()


def finish_kernel(len_ref, qx, acc, top, kvb, out_ref, kx, vx, s0, s1, ov, sem):
    reqs, rows, dim = ov.shape
    start = kvb.shape[2] - kx.shape[1]
    tile = 512
    bufs = (s0, s1)
    for j in range(reqs):
        def scores(t, j=j):
            bufs[t % 2][...] = scores_of(qx[j, pl.ds(t * tile, tile), :], kx[j])

        def put(at, number, total, j=j):
            ov[j, at, :] = (number / total).astype(ov.dtype)
            pltpu.make_async_copy(ov.at[j, at], out_ref.at[j, at], sem).start()

        @pl.when(len_ref[j] > start)
        def _(j=j, scores=scores, put=put):
            mark(start, j, len_ref, vx)
            prepare(start, j, kvb, kx, vx)
            scores(0)
            for t in range(rows // tile):
                if t + 1 < rows // tile:
                    scores(t + 1)
                at = pl.ds(t * tile, tile)
                _, fade, mixed = join(bufs[t % 2][...], top[j, at, :], vx[j])
                put(at, acc[j, at, :dim] * fade + mixed[:, :dim], acc[j, at, dim:] * fade + mixed[:, dim:])

        @pl.when(len_ref[j] <= start)
        def _(j=j, put=put):
            for t in range(rows // tile):
                at = pl.ds(t * tile, tile)
                put(at, acc[j, at, :dim], acc[j, at, dim:])

    pltpu.make_async_copy(ov, out_ref, sem).wait()


def attend(slot_of_req, cache_len, queries, stretch_keys, stretch_values, cache_keys, cache_values, n):
    vmem = pltpu.VMEM
    reqs, rows, dim = queries.shape
    span = cache_keys.shape[1]
    sizes = [span // 8 * c for c in CHUNKS]
    pieces = [vmem((2 * n, size // 2 // n, dim), queries.dtype) for size in sizes]
    wide = [vmem((reqs, size, 2 * dim), queries.dtype) for size in sizes]
    k = len(sizes)
    kind = queries.dtype
    any_spec = pl.BlockSpec(memory_space=pltpu.HBM)
    smem = pl.BlockSpec(memory_space=pltpu.SMEM)
    dma = pltpu.SemaphoreType.DMA
    held = pl.BlockSpec(memory_space=vmem)
    state = (
        vmem((reqs, rows, 2 * dim), kind),
        vmem((reqs, rows, 2 * dim), F32), vmem((reqs, rows, dim), F32),
        vmem((2, reqs, span, dim), kind),
    )
    limit = 57_600_000
    state = pl.pallas_call(
        functools.partial(kernel, n),
        out_shape=state,
        in_specs=[smem] * 2 + [any_spec] * 5,
        out_specs=(held,) * len(state),
        scratch_shapes=[
            vmem((reqs, rows, dim), kind),
            vmem((reqs, span, dim), kind), vmem((reqs, span, dim), kind),
            vmem((1024, max(sizes)), F32), vmem((1024, max(sizes)), F32),
            pieces, pieces, wide[:-1], wide[:-1],
            dma((3,)), dma((k,)), dma((3, 2)), dma((3, 2)), dma((k,)), dma((k,)), dma((k,)), dma((k, n)),
            dma((k,)), dma((k, n)), dma, dma((k,)),
        ],
        compiler_params=pltpu.CompilerParams(collective_id=0, has_side_effects=True, vmem_limit_bytes=limit),
    )(slot_of_req, cache_len, queries, stretch_keys, stretch_values, cache_keys, cache_values)
    state = [pltpu.with_memory_space_constraint(a, vmem) for a in state]
    return pl.pallas_call(
        finish_kernel,
        out_shape=jax.ShapeDtypeStruct(queries.shape, kind),
        in_specs=[smem] + [held] * len(state),
        out_specs=any_spec,
        scratch_shapes=[
            wide[-1], wide[-1],
            vmem((512, sizes[-1]), F32), vmem((512, sizes[-1]), F32),
            vmem((reqs, rows, dim), kind), dma,
        ],
        compiler_params=pltpu.CompilerParams(vmem_limit_bytes=limit),
    )(cache_len, *state)


def on_device(queries, stretch_keys, stretch_values, cache_keys, cache_values, slot_of_req, cache_len):
    reqs, stretch, heads, dim = queries.shape
    flat = [a.reshape(a.shape[0], a.shape[1], dim) for a in (stretch_keys, stretch_values, cache_keys, cache_values)]
    rows = queries.reshape(reqs, stretch * heads, dim)
    out = attend(slot_of_req, cache_len, rows, *flat, lax.axis_size("req"))
    return out.reshape(queries.shape)


def solution(mesh):
    return jax.shard_map(
        on_device,
        mesh=mesh,
        in_specs=(
            P("req", None, ("kvh", "qh"), None),
            P("req", "qh", "kvh", None),
            P("req", "qh", "kvh", None),
            P("req", None, "kvh", None),
            P("req", None, "kvh", None),
            P(),
            P("req"),
        ),
        out_specs=P("req", None, ("kvh", "qh"), None),
        check_vma=False,
    )
```

```python
import functools
import math

import jax
import jax.numpy as jnp
from jax import lax
from jax.experimental import pallas as pl
from jax.experimental.pallas import tpu as pltpu
from jax.sharding import PartitionSpec as P

MESH = pl.DeviceIdType.MESH
HIDDEN = -1e30
F32 = jnp.float32


CHUNKS = (4, 4)


def scores_of(query, keys):
    return lax.dot_general(query, keys, (((1,), (1,)), ((), ())), preferred_element_type=F32)


def mark(start, j, len_ref, vx):
    size, dim = vx.shape[1], vx.shape[2] // 2
    place = start + lax.broadcasted_iota(jnp.int32, (size, dim), 0)
    vx[j, :, dim:] = jnp.where(place < len_ref[j], 1.0, 0.0).astype(jnp.bfloat16)


def prepare(start, j, kvb, kx, vx):
    size, dim = kx.shape[1], kx.shape[2] // 2
    at = pl.ds(start, size)
    visible = vx[j, :, dim:]
    keys = kvb[0, j, at, :] * visible + kvb[0, j, 0:1, :] * (1 - visible)
    kx[j, :, :dim] = keys
    kx[j, :, dim:] = keys
    vx[j, :, :dim] = kvb[1, j, at, :] * visible


def join(scores, before, values):
    now = jnp.maximum(before, jnp.max(scores, axis=1, keepdims=True))
    wide = jnp.concatenate([now] * (scores.shape[1] // now.shape[1]), axis=1)
    weights = jnp.exp2(scores - wide).astype(jnp.bfloat16)
    return now, jnp.exp2(before - now), jnp.dot(weights, values, preferred_element_type=F32)


def kernel(
    n, slot_ref, len_ref, q_ref, sk_ref, sv_ref, ck_ref, cv_ref, qx, acc, top, kvb,
    qv, skb, svb, s0, s1, spread, picked, kx, vx,
    local_sem, own_sem, s_send, s_recv, p1_send, p1_recv, p2_send, p2_recv, x_send, x_recv, y_send, y_recv,
):
    me = lax.axis_index("req")
    q = lax.axis_index("qh")
    core = lax.rem(q, 2)
    side = q // 2
    mate = q + 1 - 2 * core
    over = lax.rem(q + 2, 4)
    reqs, rows, dim = q_ref.shape
    per = sk_ref.shape[1]
    span = ck_ref.shape[1]
    sizes = [span // 8 * c for c in CHUNKS]
    starts = [sum(sizes[:h]) for h in range(len(sizes))]
    chunks = range(len(sizes))
    depth = n // 2

    far = sorted(range(depth), key=lambda dz: -min(dz, depth - dz))
    offsets = [(dx, dz) for dz in far for dx in (1, 0) if dx or dz]
    all_offsets = offsets + [(0, 0)]
    here = side * 2 + me // depth
    up = here + 1 - 2 * lax.rem(here, 2)
    down = lax.rem(here + 3 + 2 * lax.rem(here, 2), 4)
    columns = [(x // 2, lax.rem(x, 2) * depth) for x in (here, up, down)]
    heights = [lax.rem(lax.rem(me, depth) + dz, depth) for dz in range(depth)]

    def partner(offset, sign):
        dx, dz = offset
        of_side, base = columns[dx * (1 + dz % 2)]
        return of_side, base + heights[sign * dz % depth]

    def rows_of(h, of_side, index):
        piece = sizes[h] // 2 // n
        return pl.ds(pl.multiple_of(starts[h] + (of_side * n + index) * piece, piece), piece)

    def pair(index):
        return pl.ds(2 * index, 2)

    def to_req(src, dst, send, recv, of_side, index):
        return pltpu.make_async_remote_copy(
            src, dst, send, recv, device_id={"qh": of_side * 2 + core, "req": index}, device_id_type=MESH
        )

    def to_qh(src, dst, send, recv, index):
        return pltpu.make_async_remote_copy(
            src, dst, send, recv, device_id={"qh": index}, device_id_type=MESH
        )

    barrier = pltpu.get_barrier_semaphore()
    for offset in offsets:
        of_side, index = partner(offset, 1)
        pl.semaphore_signal(
            barrier, inc=1, device_id={"qh": of_side * 2 + core, "req": index}, device_id_type=MESH
        )
    for peer in (over, mate):
        pl.semaphore_signal(barrier, inc=1, device_id={"qh": peer}, device_id_type=MESH)

    own = pl.ds(pl.multiple_of(q * per, per), per)
    load_q = pltpu.make_async_copy(q_ref, qv, local_sem.at[0])
    own_copies = [
        pltpu.make_async_copy(sk_ref, skb.at[:, own], local_sem.at[1]),
        pltpu.make_async_copy(sv_ref, svb.at[:, own], local_sem.at[2]),
    ]

    pl.semaphore_wait(barrier, n + 1)

    for c, src in enumerate((ck_ref, cv_ref)):
        @pl.when(core == c)
        def _(src=src):
            for h in chunks:
                for offset in offsets:
                    of_side, to = partner(offset, 1)
                    to_req(
                        src.at[:, rows_of(h, of_side, to)], spread[h].at[pair(me)], p1_send.at[h], p1_recv.at[h],
                        of_side, to,
                    ).start()
                pltpu.make_async_copy(
                    src.at[:, rows_of(h, side, me)], spread[h].at[pair(me)], own_sem.at[h]
                ).start()

    def stretch_to(k, peer):
        return [
            to_qh(src, dst.at[:, own], s_send.at[k, i], s_recv.at[k, i], peer)
            for i, (src, dst) in enumerate(((sk_ref, skb), (sv_ref, svb)))
        ]

    to_over = stretch_to(0, over)
    to_mate = stretch_to(1, mate)
    for copy in to_over + to_mate + [load_q] + own_copies:
        copy.start()

    scale = math.log2(math.e) / math.sqrt(dim)
    load_q.wait()
    block = 256

    def widen(i, _):
        at = pl.ds(pl.multiple_of(i * block, block), block)
        for j in range(reqs):
            value = qv[j, at, :].astype(F32) * scale
            high = value.astype(jnp.bfloat16)
            qx[j, at, :dim] = high
            qx[j, at, dim:] = (value - high.astype(F32)).astype(jnp.bfloat16)
        return 0

    lax.fori_loop(0, rows // block, widen, 0)

    most = pl.ds(0, 2 * (n - 1))

    def collect(h):
        pltpu.make_async_copy(spread[h].at[pair(me)], spread[h].at[pair(me)], own_sem.at[h]).wait()
        pltpu.make_async_copy(spread[h].at[most], spread[h].at[most], p1_recv.at[h]).wait()
        for r in range(2 * n):
            picked[h][r] = spread[h][slot_ref[r]]
        dst = kvb.at[core, :, rows_of(h, side, me)]
        for i, offset in enumerate(offsets):
            of_side, to = partner(offset, 1)
            to_req(picked[h].at[pair(to)], dst, p2_send.at[h], p2_recv.at[h, i], of_side, to).start()
        pltpu.make_async_copy(picked[h].at[pair(me)], dst, p2_recv.at[h, n - 1]).start()

    def forward(h):
        for i in reversed(range(n)):
            of_side, index = partner(all_offsets[i], -1)
            at = kvb.at[core, :, rows_of(h, of_side, index)]
            pltpu.make_async_copy(picked[h].at[pair(0)], at, p2_recv.at[h, i]).wait()
            to_qh(at, at, x_send.at[h], x_recv.at[h, i], over).start()
            to_qh(at, at, y_send, y_recv.at[h], mate).start()

    def onward(h):
        for i in reversed(range(n)):
            of_side, index = partner(all_offsets[i], -1)
            at = kvb.at[core, :, rows_of(h, 1 - of_side, index)]
            pltpu.make_async_copy(picked[h].at[pair(0)], at, x_recv.at[h, i]).wait()
            to_qh(at, at, y_send, y_recv.at[h], mate).start()

    tile = 512
    tokens = tile // 2

    def stretch_attention(j):
        for i in range(rows // tile):
            at = pl.ds(i * tile, tile)
            seen = (i + 1) * tokens
            keys = skb[j, :seen, :]
            scores = scores_of(qx[j, at, :], jnp.concatenate([keys, keys], axis=1))
            row = lax.broadcasted_iota(jnp.int32, (tile, tokens), 0) // 2
            col = lax.broadcasted_iota(jnp.int32, (tile, tokens), 1)
            last = jnp.where(col <= row, scores[:, seen - tokens:], HIDDEN)
            scores = jnp.concatenate([scores[:, : seen - tokens], last], axis=1) if i else last
            highest = jnp.max(scores, axis=1, keepdims=True)
            weights = jnp.exp2(scores - highest).astype(jnp.bfloat16)
            values = svb[j, :seen, :]
            wide = jnp.concatenate([values, jnp.ones_like(values)], axis=1)
            acc[j, at, :] = jnp.dot(weights, wide, preferred_element_type=F32)
            top[j, at, :] = jnp.broadcast_to(highest, (tile, dim))

    big = 1024
    count = reqs * rows // big

    def place_of(t):
        return t // (rows // big), pl.ds(t % (rows // big) * big, big)

    def cached_scores(h, t):
        j, at = place_of(t)
        (s0, s1)[t % 2][:, : sizes[h]] = scores_of(qx[j, at, :], kx[h][j])

    def cached_attention(h, first, stop):
        for t in range(first, stop):
            if t + 1 < count:
                cached_scores(h, t + 1)
            j, at = place_of(t)
            now, fade, mixed = join((s0, s1)[t % 2][:, : sizes[h]], top[j, at, :], vx[h][j])
            acc[j, at, :dim] = acc[j, at, :dim] * fade + mixed[:, :dim]
            acc[j, at, dim:] = acc[j, at, dim:] * fade + mixed[:, dim:]
            top[j, at, :] = now

    for h in chunks[:-1]:
        for j in range(reqs):
            mark(starts[h], j, len_ref, vx[h])
    collect(0)
    for copy in to_over:
        copy.wait_recv()
    theirs = pl.ds(pl.multiple_of(over * per, per), per)
    passed = [
        to_qh(dst.at[:, theirs], dst.at[:, theirs], s_send.at[2, i], s_recv.at[2, i], mate)
        for i, dst in enumerate((skb, svb))
    ]
    for copy in passed:
        copy.start()
    for h in chunks[1:]:
        collect(h)
    for copy in own_copies:
        copy.wait()
    for copy in to_mate + passed:
        copy.wait_recv()
    stretch_attention(0)
    forward(0)
    stretch_attention(1)
    for h in chunks[1:]:
        forward(h)
    onward(0)
    for h in chunks:
        landed = kvb.at[0, :, pl.ds(starts[h], sizes[h])]
        pltpu.make_async_copy(landed, landed, y_recv.at[h]).wait()
        if h == chunks[-1]:
            break
        for j in range(reqs):
            prepare(starts[h], j, kvb, kx[h], vx[h])
        cached_scores(h, 0)
        cached_attention(h, 0, count // 2)
        onward(h + 1)
        cached_attention(h, count // 2, count)

    for copy in to_over + to_mate + passed:
        copy.wait_send()
    for sem in (p1_send, p2_send):
        for h in chunks:
            pltpu.make_async_copy(picked[h].at[most], picked[h].at[most], sem.at[h]).wait()
    for h in chunks:
        pltpu.make_async_copy(picked[h], picked[h], x_send.at[h]).wait()
    pltpu.make_async_copy(kvb.at[0], kvb.at[0], y_send).wait()


def finish_kernel(len_ref, qx, acc, top, kvb, out_ref, kx, vx, s0, s1, ov, sem):
    reqs, rows, dim = ov.shape
    start = kvb.shape[2] - kx.shape[1]
    tile = 512
    bufs = (s0, s1)
    step = kx.shape[1] // 2

    def put(j, at, number, total):
        ov[j, at, :] = (number / total).astype(ov.dtype)
        pltpu.make_async_copy(ov.at[j, at], out_ref.at[j, at], sem).start()

    def divide(j):
        for t in range(rows // tile):
            at = pl.ds(t * tile, tile)
            put(j, at, acc[j, at, :dim], acc[j, at, dim:])

    def attend_to(size, j):
        keys, values = kx.at[:, pl.ds(0, size)], vx.at[:, pl.ds(0, size)]

        def scores(t):
            bufs[t % 2][:, :size] = scores_of(qx[j, pl.ds(t * tile, tile), :], keys[j])

        mark(start, j, len_ref, values)
        prepare(start, j, kvb, keys, values)
        scores(0)
        for t in range(rows // tile):
            if t + 1 < rows // tile:
                scores(t + 1)
            at = pl.ds(t * tile, tile)
            _, fade, mixed = join(bufs[t % 2][:, :size], top[j, at, :], values[j])
            put(j, at, acc[j, at, :dim] * fade + mixed[:, :dim], acc[j, at, dim:] * fade + mixed[:, dim:])

    for j in range(reqs):
        length = len_ref[j]
        pl.when(length <= start)(functools.partial(divide, j))
        pl.when((length > start) & (length <= start + step))(functools.partial(attend_to, step, j))
        pl.when(length > start + step)(functools.partial(attend_to, 2 * step, j))

    pltpu.make_async_copy(ov, out_ref, sem).wait()


def attend(slot_of_req, cache_len, queries, stretch_keys, stretch_values, cache_keys, cache_values, n):
    vmem = pltpu.VMEM
    reqs, rows, dim = queries.shape
    span = cache_keys.shape[1]
    sizes = [span // 8 * c for c in CHUNKS]
    pieces = [vmem((2 * n, size // 2 // n, dim), queries.dtype) for size in sizes]
    wide = [vmem((reqs, size, 2 * dim), queries.dtype) for size in sizes]
    k = len(sizes)
    kind = queries.dtype
    any_spec = pl.BlockSpec(memory_space=pltpu.HBM)
    smem = pl.BlockSpec(memory_space=pltpu.SMEM)
    dma = pltpu.SemaphoreType.DMA
    held = pl.BlockSpec(memory_space=vmem)
    state = (
        vmem((reqs, rows, 2 * dim), kind),
        vmem((reqs, rows, 2 * dim), F32), vmem((reqs, rows, dim), F32),
        vmem((2, reqs, span, dim), kind),
    )
    limit = 57_600_000
    state = pl.pallas_call(
        functools.partial(kernel, n),
        out_shape=state,
        in_specs=[smem] * 2 + [any_spec] * 5,
        out_specs=(held,) * len(state),
        scratch_shapes=[
            vmem((reqs, rows, dim), kind),
            vmem((reqs, span, dim), kind), vmem((reqs, span, dim), kind),
            vmem((1024, max(sizes)), F32), vmem((1024, max(sizes)), F32),
            pieces, pieces, wide[:-1], wide[:-1],
            dma((3,)), dma((k,)), dma((3, 2)), dma((3, 2)), dma((k,)), dma((k,)), dma((k,)), dma((k, n)),
            dma((k,)), dma((k, n)), dma, dma((k,)),
        ],
        compiler_params=pltpu.CompilerParams(collective_id=0, has_side_effects=True, vmem_limit_bytes=limit),
    )(slot_of_req, cache_len, queries, stretch_keys, stretch_values, cache_keys, cache_values)
    state = [pltpu.with_memory_space_constraint(a, vmem) for a in state]
    return pl.pallas_call(
        finish_kernel,
        out_shape=jax.ShapeDtypeStruct(queries.shape, kind),
        in_specs=[smem] + [held] * len(state),
        out_specs=any_spec,
        scratch_shapes=[
            wide[-1], wide[-1],
            vmem((512, sizes[-1]), F32), vmem((512, sizes[-1]), F32),
            vmem((reqs, rows, dim), kind), dma,
        ],
        compiler_params=pltpu.CompilerParams(vmem_limit_bytes=limit),
    )(cache_len, *state)


def on_device(queries, stretch_keys, stretch_values, cache_keys, cache_values, slot_of_req, cache_len):
    reqs, stretch, heads, dim = queries.shape
    flat = [a.reshape(a.shape[0], a.shape[1], dim) for a in (stretch_keys, stretch_values, cache_keys, cache_values)]
    rows = queries.reshape(reqs, stretch * heads, dim)
    out = attend(slot_of_req, cache_len, rows, *flat, lax.axis_size("req"))
    return out.reshape(queries.shape)


def solution(mesh):
    return jax.shard_map(
        on_device,
        mesh=mesh,
        in_specs=(
            P("req", None, ("kvh", "qh"), None),
            P("req", "qh", "kvh", None),
            P("req", "qh", "kvh", None),
            P("req", None, "kvh", None),
            P("req", None, "kvh", None),
            P(),
            P("req"),
        ),
        out_specs=P("req", None, ("kvh", "qh"), None),
        check_vma=False,
    )
```

```python
import functools
import math

import jax
import jax.numpy as jnp
from jax import lax
from jax.experimental import pallas as pl
from jax.experimental.pallas import tpu as pltpu
from jax.sharding import PartitionSpec as P

MESH = pl.DeviceIdType.MESH
HIDDEN = -1e30
F32 = jnp.float32


CHUNKS = (4, 4)


def scores_of(query, keys):
    return lax.dot_general(query, keys, (((1,), (1,)), ((), ())), preferred_element_type=F32)


def mark(start, j, len_ref, vx):
    size, dim = vx.shape[1], vx.shape[2] // 2
    place = start + lax.broadcasted_iota(jnp.int32, (size, dim), 0)
    vx[j, :, dim:] = jnp.where(place < len_ref[j], 1.0, 0.0).astype(jnp.bfloat16)


def prepare(start, j, kvb, kx, vx):
    size, dim = kx.shape[1], kx.shape[2] // 2
    at = pl.ds(start, size)
    visible = vx[j, :, dim:]
    keys = kvb[0, j, at, :] * visible + kvb[0, j, 0:1, :] * (1 - visible)
    kx[j, :, :dim] = keys
    kx[j, :, dim:] = keys
    vx[j, :, :dim] = kvb[1, j, at, :] * visible


def join(scores, before, values):
    now = jnp.maximum(before, jnp.max(scores, axis=1, keepdims=True))
    wide = jnp.concatenate([now] * (scores.shape[1] // now.shape[1]), axis=1)
    weights = jnp.exp2(scores - wide).astype(jnp.bfloat16)
    return now, jnp.exp2(before - now), jnp.dot(weights, values, preferred_element_type=F32)


def kernel(
    n, slot_ref, len_ref, q_ref, sk_ref, sv_ref, ck_ref, cv_ref, qx, acc, top, kvb,
    qv, skb, svb, s0, s1, spread, picked, kx, vx,
    local_sem, own_sem, s_send, s_recv, p1_send, p1_recv, p2_send, p2_recv, x_send, x_recv, y_send, y_recv,
):
    me = lax.axis_index("req")
    q = lax.axis_index("qh")
    core = lax.rem(q, 2)
    side = q // 2
    mate = q + 1 - 2 * core
    over = lax.rem(q + 2, 4)
    reqs, rows, dim = q_ref.shape
    per = sk_ref.shape[1]
    span = ck_ref.shape[1]
    sizes = [span // 8 * c for c in CHUNKS]
    starts = [sum(sizes[:h]) for h in range(len(sizes))]
    chunks = range(len(sizes))
    depth = n // 2

    far = sorted(range(depth), key=lambda dz: -min(dz, depth - dz))
    offsets = [(dx, dz) for dz in far for dx in (1, 0) if dx or dz]
    all_offsets = offsets + [(0, 0)]
    here = side * 2 + me // depth
    up = here + 1 - 2 * lax.rem(here, 2)
    down = lax.rem(here + 3 + 2 * lax.rem(here, 2), 4)
    columns = [(x // 2, lax.rem(x, 2) * depth) for x in (here, up, down)]
    heights = [lax.rem(lax.rem(me, depth) + dz, depth) for dz in range(depth)]

    def partner(offset, sign):
        dx, dz = offset
        of_side, base = columns[dx * (1 + dz % 2)]
        return of_side, base + heights[sign * dz % depth]

    def rows_of(h, of_side, index):
        piece = sizes[h] // 2 // n
        return pl.ds(pl.multiple_of(starts[h] + (of_side * n + index) * piece, piece), piece)

    def pair(index):
        return pl.ds(2 * index, 2)

    def to_req(src, dst, send, recv, of_side, index):
        return pltpu.make_async_remote_copy(
            src, dst, send, recv, device_id={"qh": of_side * 2 + core, "req": index}, device_id_type=MESH
        )

    def to_qh(src, dst, send, recv, index):
        return pltpu.make_async_remote_copy(
            src, dst, send, recv, device_id={"qh": index}, device_id_type=MESH
        )

    barrier = pltpu.get_barrier_semaphore()
    for offset in offsets:
        of_side, index = partner(offset, 1)
        pl.semaphore_signal(
            barrier, inc=1, device_id={"qh": of_side * 2 + core, "req": index}, device_id_type=MESH
        )
    for peer in (over, mate):
        pl.semaphore_signal(barrier, inc=1, device_id={"qh": peer}, device_id_type=MESH)

    own = pl.ds(pl.multiple_of(q * per, per), per)
    load_q = pltpu.make_async_copy(q_ref, qv, local_sem.at[0])
    own_copies = [
        pltpu.make_async_copy(sk_ref, skb.at[:, own], local_sem.at[1]),
        pltpu.make_async_copy(sv_ref, svb.at[:, own], local_sem.at[2]),
    ]

    pl.semaphore_wait(barrier, n + 1)

    for c, src in enumerate((ck_ref, cv_ref)):
        @pl.when(core == c)
        def _(src=src):
            for h in chunks:
                for offset in offsets:
                    of_side, to = partner(offset, 1)
                    to_req(
                        src.at[:, rows_of(h, of_side, to)], spread[h].at[pair(me)], p1_send.at[h], p1_recv.at[h],
                        of_side, to,
                    ).start()
                pltpu.make_async_copy(
                    src.at[:, rows_of(h, side, me)], spread[h].at[pair(me)], own_sem.at[h]
                ).start()

    def stretch_to(k, peer):
        return [
            to_qh(src, dst.at[:, own], s_send.at[k, i], s_recv.at[k, i], peer)
            for i, (src, dst) in enumerate(((sk_ref, skb), (sv_ref, svb)))
        ]

    to_over = stretch_to(0, over)
    to_mate = stretch_to(1, mate)
    for copy in to_over + to_mate + [load_q] + own_copies:
        copy.start()

    scale = math.log2(math.e) / math.sqrt(dim)
    load_q.wait()
    block = 512

    def widen(i, _):
        at = pl.ds(pl.multiple_of(i * block, block), block)
        for j in range(reqs):
            value = qv[j, at, :].astype(F32) * scale
            high = value.astype(jnp.bfloat16)
            qx[j, at, :dim] = high
            qx[j, at, dim:] = (value - high.astype(F32)).astype(jnp.bfloat16)
        return 0

    lax.fori_loop(0, rows // block, widen, 0)

    most = pl.ds(0, 2 * (n - 1))

    def collect(h):
        pltpu.make_async_copy(spread[h].at[pair(me)], spread[h].at[pair(me)], own_sem.at[h]).wait()
        pltpu.make_async_copy(spread[h].at[most], spread[h].at[most], p1_recv.at[h]).wait()
        for r in range(2 * n):
            picked[h][r] = spread[h][slot_ref[r]]
        dst = kvb.at[core, :, rows_of(h, side, me)]
        for i, offset in enumerate(offsets):
            of_side, to = partner(offset, 1)
            to_req(picked[h].at[pair(to)], dst, p2_send.at[h], p2_recv.at[h, i], of_side, to).start()
        pltpu.make_async_copy(picked[h].at[pair(me)], dst, p2_recv.at[h, n - 1]).start()

    def forward(h):
        for i in reversed(range(n)):
            of_side, index = partner(all_offsets[i], -1)
            at = kvb.at[core, :, rows_of(h, of_side, index)]
            pltpu.make_async_copy(picked[h].at[pair(0)], at, p2_recv.at[h, i]).wait()
            to_qh(at, at, x_send.at[h], x_recv.at[h, i], over).start()
            to_qh(at, at, y_send, y_recv.at[h], mate).start()

    def onward(h):
        for i in reversed(range(n)):
            of_side, index = partner(all_offsets[i], -1)
            at = kvb.at[core, :, rows_of(h, 1 - of_side, index)]
            pltpu.make_async_copy(picked[h].at[pair(0)], at, x_recv.at[h, i]).wait()
            to_qh(at, at, y_send, y_recv.at[h], mate).start()

    tile = 512
    tokens = tile // 2

    def stretch_attention(j):
        for i in range(rows // tile):
            at = pl.ds(i * tile, tile)
            seen = (i + 1) * tokens
            keys = skb[j, :seen, :]
            scores = scores_of(qx[j, at, :], jnp.concatenate([keys, keys], axis=1))
            row = lax.broadcasted_iota(jnp.int32, (tile, tokens), 0) // 2
            col = lax.broadcasted_iota(jnp.int32, (tile, tokens), 1)
            last = jnp.where(col <= row, scores[:, seen - tokens:], HIDDEN)
            scores = jnp.concatenate([scores[:, : seen - tokens], last], axis=1) if i else last
            highest = jnp.broadcast_to(jnp.max(scores, axis=1, keepdims=True), (tile, dim))
            spread_top = jnp.concatenate([highest] * (seen // dim), axis=1)
            weights = jnp.exp2(scores - spread_top).astype(jnp.bfloat16)
            values = svb[j, :seen, :]
            wide = jnp.concatenate([values, jnp.ones_like(values)], axis=1)
            acc[j, at, :] = jnp.dot(weights, wide, preferred_element_type=F32)
            top[j, at, :] = highest

    big = 1024
    count = reqs * rows // big

    def place_of(t):
        return t // (rows // big), pl.ds(t % (rows // big) * big, big)

    def cached_scores(h, t):
        j, at = place_of(t)
        (s0, s1)[t % 2][:, : sizes[h]] = scores_of(qx[j, at, :], kx[h][j])

    def cached_attention(h, first, stop):
        for t in range(first, stop):
            if t + 1 < count:
                cached_scores(h, t + 1)
            j, at = place_of(t)
            now, fade, mixed = join((s0, s1)[t % 2][:, : sizes[h]], top[j, at, :], vx[h][j])
            acc[j, at, :dim] = acc[j, at, :dim] * fade + mixed[:, :dim]
            acc[j, at, dim:] = acc[j, at, dim:] * fade + mixed[:, dim:]
            top[j, at, :] = now

    for h in chunks[:-1]:
        for j in range(reqs):
            mark(starts[h], j, len_ref, vx[h])
    collect(0)
    for copy in to_over:
        copy.wait_recv()
    theirs = pl.ds(pl.multiple_of(over * per, per), per)
    passed = [
        to_qh(dst.at[:, theirs], dst.at[:, theirs], s_send.at[2, i], s_recv.at[2, i], mate)
        for i, dst in enumerate((skb, svb))
    ]
    for copy in passed:
        copy.start()
    for h in chunks[1:]:
        collect(h)
    for copy in own_copies:
        copy.wait()
    for copy in to_mate + passed:
        copy.wait_recv()
    stretch_attention(0)
    forward(0)
    stretch_attention(1)
    for h in chunks[1:]:
        forward(h)
    onward(0)
    for h in chunks:
        landed = kvb.at[0, :, pl.ds(starts[h], sizes[h])]
        pltpu.make_async_copy(landed, landed, y_recv.at[h]).wait()
        if h == chunks[-1]:
            break
        for j in range(reqs):
            prepare(starts[h], j, kvb, kx[h], vx[h])
        cached_scores(h, 0)
        cached_attention(h, 0, count // 2)
        onward(h + 1)
        cached_attention(h, count // 2, count)

    for copy in to_over + to_mate + passed:
        copy.wait_send()
    for sem in (p1_send, p2_send):
        for h in chunks:
            pltpu.make_async_copy(picked[h].at[most], picked[h].at[most], sem.at[h]).wait()
    for h in chunks:
        pltpu.make_async_copy(picked[h], picked[h], x_send.at[h]).wait()
    pltpu.make_async_copy(kvb.at[0], kvb.at[0], y_send).wait()


def finish_kernel(len_ref, qx, acc, top, kvb, out_ref, kx, vx, s0, s1, ov, sem):
    reqs, rows, dim = ov.shape
    start = kvb.shape[2] - kx.shape[1]
    tile = 512
    bufs = (s0, s1)
    step = kx.shape[1] // 2

    def put(j, at, number, total):
        ov[j, at, :] = (number / total).astype(ov.dtype)
        pltpu.make_async_copy(ov.at[j, at], out_ref.at[j, at], sem).start()

    def divide(j):
        for t in range(rows // tile):
            at = pl.ds(t * tile, tile)
            put(j, at, acc[j, at, :dim], acc[j, at, dim:])

    def attend_to(size, j):
        keys, values = kx.at[:, pl.ds(0, size)], vx.at[:, pl.ds(0, size)]

        def scores(t):
            bufs[t % 2][:, :size] = scores_of(qx[j, pl.ds(t * tile, tile), :], keys[j])

        mark(start, j, len_ref, values)
        prepare(start, j, kvb, keys, values)
        scores(0)
        for t in range(rows // tile):
            if t + 1 < rows // tile:
                scores(t + 1)
            at = pl.ds(t * tile, tile)
            _, fade, mixed = join(bufs[t % 2][:, :size], top[j, at, :], values[j])
            put(j, at, acc[j, at, :dim] * fade + mixed[:, :dim], acc[j, at, dim:] * fade + mixed[:, dim:])

    for j in range(reqs):
        length = len_ref[j]
        pl.when(length <= start)(functools.partial(divide, j))
        pl.when((length > start) & (length <= start + step))(functools.partial(attend_to, step, j))
        pl.when(length > start + step)(functools.partial(attend_to, 2 * step, j))

    pltpu.make_async_copy(ov, out_ref, sem).wait()


def attend(slot_of_req, cache_len, queries, stretch_keys, stretch_values, cache_keys, cache_values, n):
    vmem = pltpu.VMEM
    reqs, rows, dim = queries.shape
    span = cache_keys.shape[1]
    sizes = [span // 8 * c for c in CHUNKS]
    pieces = [vmem((2 * n, size // 2 // n, dim), queries.dtype) for size in sizes]
    wide = [vmem((reqs, size, 2 * dim), queries.dtype) for size in sizes]
    k = len(sizes)
    kind = queries.dtype
    any_spec = pl.BlockSpec(memory_space=pltpu.HBM)
    smem = pl.BlockSpec(memory_space=pltpu.SMEM)
    dma = pltpu.SemaphoreType.DMA
    held = pl.BlockSpec(memory_space=vmem)
    state = (
        vmem((reqs, rows, 2 * dim), kind),
        vmem((reqs, rows, 2 * dim), F32), vmem((reqs, rows, dim), F32),
        vmem((2, reqs, span, dim), kind),
    )
    limit = 57_600_000
    state = pl.pallas_call(
        functools.partial(kernel, n),
        out_shape=state,
        in_specs=[smem] * 2 + [any_spec] * 5,
        out_specs=(held,) * len(state),
        scratch_shapes=[
            vmem((reqs, rows, dim), kind),
            vmem((reqs, span, dim), kind), vmem((reqs, span, dim), kind),
            vmem((1024, max(sizes)), F32), vmem((1024, max(sizes)), F32),
            pieces, pieces, wide[:-1], wide[:-1],
            dma((3,)), dma((k,)), dma((3, 2)), dma((3, 2)), dma((k,)), dma((k,)), dma((k,)), dma((k, n)),
            dma((k,)), dma((k, n)), dma, dma((k,)),
        ],
        compiler_params=pltpu.CompilerParams(collective_id=0, has_side_effects=True, vmem_limit_bytes=limit),
    )(slot_of_req, cache_len, queries, stretch_keys, stretch_values, cache_keys, cache_values)
    state = [pltpu.with_memory_space_constraint(a, vmem) for a in state]
    return pl.pallas_call(
        finish_kernel,
        out_shape=jax.ShapeDtypeStruct(queries.shape, kind),
        in_specs=[smem] + [held] * len(state),
        out_specs=any_spec,
        scratch_shapes=[
            wide[-1], wide[-1],
            vmem((512, sizes[-1]), F32), vmem((512, sizes[-1]), F32),
            vmem((reqs, rows, dim), kind), dma,
        ],
        compiler_params=pltpu.CompilerParams(vmem_limit_bytes=limit),
    )(cache_len, *state)


def on_device(queries, stretch_keys, stretch_values, cache_keys, cache_values, slot_of_req, cache_len):
    reqs, stretch, heads, dim = queries.shape
    flat = [a.reshape(a.shape[0], a.shape[1], dim) for a in (stretch_keys, stretch_values, cache_keys, cache_values)]
    rows = queries.reshape(reqs, stretch * heads, dim)
    out = attend(slot_of_req, cache_len, rows, *flat, lax.axis_size("req"))
    return out.reshape(queries.shape)


def solution(mesh):
    return jax.shard_map(
        on_device,
        mesh=mesh,
        in_specs=(
            P("req", None, ("kvh", "qh"), None),
            P("req", "qh", "kvh", None),
            P("req", "qh", "kvh", None),
            P("req", None, "kvh", None),
            P("req", None, "kvh", None),
            P(),
            P("req"),
        ),
        out_specs=P("req", None, ("kvh", "qh"), None),
        check_vma=False,
    )
```
